128 devices in a mesh: ctx: 16 (over y_hi, z, core), head: 8 (over x, y_lo).
Axes of the slice: x: 4, y: 4 (y_hi: 2, y_lo: 2; y = y_hi * 2 + y_lo), z: 4, core: 2. Of those that a mesh axis runs over, the one named last changes fastest.
Arguments:
- queries: bfloat16 [4096, 8192], P('ctx', 'head'), may hold values from -40 to 40
- keys: bfloat16 [4096, 1024], P('ctx', 'head'), may hold values from -4 to 4
- values: bfloat16 [4096, 1024], P('ctx', 'head'), may hold values from -6 to 6
- out_weight: bfloat16 [8192, 8192], P(None, 'head'), may hold values from -0.1796875 to 0.1796875
- doc_lengths: int32 [16], replicated, may hold values from 1 to 1024, 4096 in all
- owners: int32 [128, 1], replicated, may hold values from 0 to 15; in each aligned block of 8 rows (0 to 7, 8 to 15, ...) no two rows name the same one
Outputs:
- attended: bfloat16 [8192, 8192], P('head', 'ctx')
The draws below stay inside these ranges and needn't reach their ends.
Inputs may be any that keep to these rules, and one draw needn't show every extreme that they name: `owners`: among the 8 pieces loaded by one index of ctx (aligned blocks of 8 rows) every owner appears at most once. `doc_lengths`: the lengths sum to 4096; the longest is exactly 1024.
All inputs are finite; a program needn't handle non-finite values.
Results may differ from the reference program's by a relative error of at most 0.018.
Values may be sent and summed in bfloat16 or wider, within the bound.
A program may use at most 128 MiB of HBM per device.

```python
import math
import jax
import jax.numpy as jnp
import numpy as np
from jax import lax

D = 8192
QUERY_HEAD_COUNT = 64
KEY_VALUE_HEADS = 8
HEAD_SIZE = 128
PIECES = 8
NDOC = 16
PACKED_TOKENS = 4096
PIECE = 32
QW = 8192
KW = 1024
N_CTX = 16
N_HEAD = 8


def closing_keys(key):
    start_offset = jax.random.fold_in(key, 7)
    lookup_grid = jnp.clip(jax.random.normal(start_offset, (PACKED_TOKENS, KW), jnp.float32), -4.0, 4.0)
    return lookup_grid


def draw_keys(key, part):
    return closing_keys(key).astype(jnp.bfloat16)


def draw_queries(key, part):
    group_length = QUERY_HEAD_COUNT // KEY_VALUE_HEADS
    start_offset = jax.random.fold_in(key, 5)
    lookup_grid = jnp.clip(1.5 * jax.random.normal(start_offset, (PACKED_TOKENS, KEY_VALUE_HEADS, group_length, HEAD_SIZE), jnp.float32), -6.0, 6.0)
    return lookup_grid.reshape(PACKED_TOKENS, QUERY_HEAD_COUNT * HEAD_SIZE).astype(jnp.bfloat16)


def steps_of(stream_key, extent, pieces, smallest, high):
    gain, own = 1.0, jax.random.fold_in(stream_key, 6)
    for axis_at, blocks in pieces:
        heights = jnp.exp(jax.random.uniform(jax.random.fold_in(own, axis_at), (blocks,), jnp.float32, smallest / len(pieces), high / len(pieces)))
        gain = gain * jnp.repeat(heights, extent[axis_at] // blocks).reshape([-1 if axis == axis_at else 1 for axis in range(len(extent))])
    return gain


def profile(number_of, total, limit, skew):
    weights = [(1 << 20) // math.isqrt(grade ** skew) + 1 for grade in range(2, number_of + 1)]
    rest, counts = total - limit - (number_of - 1), [1] * (number_of - 1)
    while rest > 0:
        movable = [i for i in range(number_of - 1) if counts[i] < limit]
        whole, budget = sum([weights[i] for i in movable]), rest
        for i in movable:
            more = min(limit - counts[i], max(1, budget * weights[i] // whole), rest)
            counts[i] = counts[i] + more
            rest = rest - more
    return np.array([limit] + counts)


def ragged_sizes(own_key, amount, total, reach, skew):
    if amount == 2:
        one = jax.random.randint(own_key, (), max(1, total - reach), min(reach, total - 1) + 1)
        return jnp.stack([one, total - one])
    lengths = jnp.asarray(profile(amount, total, reach, skew), jnp.int32)
    couples = (amount - 1) // 2
    source_of, sink = lengths[1:1 + 2 * couples:2], lengths[2:2 + 2 * couples:2]
    room = jnp.minimum(source_of - 1, reach - sink)
    moved = jax.random.randint(jax.random.fold_in(own_key, 1), (couples,), 0, 1 << 20) % (room + 1)
    lengths = lengths.at[1:1 + 2 * couples:2].set(source_of - moved).at[2:2 + 2 * couples:2].set(sink + moved)
    return lengths[jax.random.permutation(jax.random.fold_in(own_key, 2), amount)]


def assign_block(rng, own, number, rows, amount, top, most, skew):
    ranking = jax.random.permutation(rng, amount)
    crowded, ordinary = portions_of(amount, rows * top, most, skew, True), portions_of(amount, rows * top, most, skew, False)
    places = jnp.arange(amount)

    def named(sizes, offset_by):
        used = int((sizes > 0).sum())
        fixed = max(1, used // 4)
        moved = fixed + (places - fixed + offset_by * (used - fixed)) % max(1, amount - fixed)
        return jnp.zeros((amount,), jnp.int32).at[ranking[jnp.where(places < fixed, places, moved)]].set(jnp.asarray(sizes, jnp.int32))

    sizes = jnp.where(number % 4 == 0, named(crowded, number // 4), named(ordinary, number - number // 4 - 1))
    mixed = jax.random.permutation(jax.random.fold_in(own, 3), amount)
    source_of, taker = mixed[0:amount // 2 * 2:2], mixed[1:amount // 2 * 2:2]
    margin = jnp.minimum(sizes[source_of] - 1, most - sizes[taker]) // 2
    margin = jnp.where((source_of == ranking[0]) | (taker == ranking[0]) | (sizes[taker] == 0), 0, jnp.maximum(margin, 0))
    moved = jax.random.randint(jax.random.fold_in(own, 4), (amount // 2,), 0, 1 << 20) % (margin + 1)
    sizes = sizes.at[source_of].add(-moved).at[taker].add(moved)
    members = jnp.searchsorted(jnp.cumsum(sizes), jnp.arange(rows * top), side="right").astype(jnp.int32)
    listing = members.reshape(top, rows).T
    listing = listing[jax.random.permutation(jax.random.fold_in(own, 1), rows)]
    offset_by = jax.random.randint(jax.random.fold_in(own, 2), (rows, 1), 0, top)
    return jnp.take_along_axis(listing, (jnp.arange(top)[None, :] + offset_by) % top, axis=1)


def portions_of(number_of, total, limit, lean, full):
    portions = [(1 << 20) // math.isqrt(standing ** lean) + 1 for standing in range(1, number_of + 1)]
    largest = limit if full else min(limit, max(-(-total // number_of), total * portions[0] // sum(portions)))
    least = 1 if total - largest >= number_of - 1 else 0
    holding, rest = [largest] + [least] * (number_of - 1), total - largest - least * (number_of - 1)
    while rest > 0:
        movable = [i for i in range(1, number_of) if holding[i] < largest] or [i for i in range(1, number_of) if holding[i] < limit]
        pool, left = sum([portions[i] for i in movable]), rest
        for i in movable:
            more = min(limit - holding[i], max(1, left * portions[i] // pool), rest)
            holding[i] = holding[i] + more
            rest = rest - more
    return np.array(holding)


def gaussian(rng, shape, deviation, limit, pieces=(), held_as=jnp.bfloat16):
    entries = deviation * jax.random.normal(rng, shape, jnp.float32)
    if pieces:
        entries = entries * steps_of(rng, shape, pieces, -0.22, 0.18)
    return jnp.clip(entries, -limit, limit).astype(held_as)


def setup_inputs(seed: int = 0) -> dict:
    key_of = jax.random.split(jax.random.key(seed), 7)
    queries = draw_queries(jax.random.fold_in(key_of[6], 71), 0)
    keys = draw_keys(jax.random.fold_in(key_of[6], 71), 0)
    values = gaussian(key_of[2], (PACKED_TOKENS, KW), 1.0, 6.0, ((0, 16), (1, 8)))
    out_weight = gaussian(key_of[3], (D, QW), 0.03, 0.1796875, ((1, 8),))
    doc_lengths = ragged_sizes(key_of[4], NDOC, PACKED_TOKENS, PACKED_TOKENS // 4, 2).astype(jnp.int32)
    owners_keys = jax.random.split(jax.random.fold_in(key_of[5], 1), (PIECES * N_CTX) // PIECES)
    owners_turns = jax.random.permutation(jax.random.fold_in(key_of[5], 3), (PIECES * N_CTX) // PIECES)
    owners = jax.vmap(lambda own, number: assign_block(jax.random.fold_in(key_of[5], 2), own, number, PIECES, N_CTX, 1, 1, 2))(owners_keys, owners_turns).reshape((PIECES * N_CTX, 1))
    return {"queries": queries, "keys": keys, "values": values, "out_weight": out_weight, "doc_lengths": doc_lengths, "owners": owners}


MASKED = -1e+30

def document_index(positions, doc_starts):
    return lax.optimization_barrier(jnp.sum((positions[:, None] >= doc_starts[None, :]).astype(jnp.int32), axis=1)) - 1

def reference(queries, keys, values, out_weight, doc_lengths, owners):
    total_rows = queries.shape[0]
    group_length = QUERY_HEAD_COUNT // KEY_VALUE_HEADS
    positions = jnp.arange(total_rows, dtype=jnp.int32)
    doc_ends = jnp.cumsum(doc_lengths).astype(jnp.int32)
    doc_starts = doc_ends - doc_lengths
    doc_ids = document_index(positions, doc_starts)
    allowed = (doc_ids[:, None] == doc_ids[None, :]) & (positions[None, :] <= positions[:, None])
    score_scale = 1.0 / math.sqrt(HEAD_SIZE)

    def one_head(head):
        query_head = lax.dynamic_slice_in_dim(queries, head * HEAD_SIZE, HEAD_SIZE, 1)
        key_head = lax.dynamic_slice_in_dim(keys, head // group_length * HEAD_SIZE, HEAD_SIZE, 1)
        value_head = lax.dynamic_slice_in_dim(values, head // group_length * HEAD_SIZE, HEAD_SIZE, 1)
        scores = lax.dot_general(query_head, key_head, (((1,), (1,)), ((), ())), preferred_element_type=jnp.float32) * score_scale
        scores = jnp.where(allowed, scores, MASKED)
        shifted = jnp.exp(scores - lax.optimization_barrier(jnp.max(scores, axis=1, keepdims=True)))
        shifted = jnp.where(allowed, shifted, 0.0)
        weights = (shifted / lax.optimization_barrier(jnp.sum(shifted, axis=1, keepdims=True))).astype(jnp.bfloat16)
        return jnp.dot(weights, value_head, preferred_element_type=jnp.float32).astype(jnp.bfloat16)
    heads_out = lax.map(one_head, jnp.arange(QUERY_HEAD_COUNT, dtype=jnp.int32))
    context = jnp.transpose(heads_out, (1, 0, 2)).reshape(total_rows, QUERY_HEAD_COUNT * HEAD_SIZE)
    group_width = QUERY_HEAD_COUNT * HEAD_SIZE // N_HEAD

    def add_group(summed, group_index):
        context_part = lax.dynamic_slice_in_dim(context, group_index * group_width, group_width, 1)
        weight_part = lax.dynamic_slice_in_dim(out_weight, group_index * group_width, group_width, 1)
        partial_sum = lax.dot_general(weight_part, context_part, (((1,), (1,)), ((), ())), preferred_element_type=jnp.float32)
        rounded = lax.optimization_barrier(partial_sum.astype(jnp.bfloat16))
        return (summed + rounded.astype(jnp.float32), None)
    summed, unused = lax.scan(add_group, jnp.zeros((D, total_rows), jnp.float32), jnp.arange(N_HEAD, dtype=jnp.int32))
    projected = summed.astype(jnp.bfloat16)
    owner_table = owners[:, 0].reshape(N_CTX, PIECES)
    owner_ids = jnp.arange(N_CTX, dtype=jnp.int32)
    slot_hits = (owner_table[None, :, :] == owner_ids[:, None, None]).astype(jnp.int32)
    slot_live = lax.optimization_barrier(jnp.sum(slot_hits, axis=2)) > 0
    picked = lax.optimization_barrier(jnp.sum(slot_hits * jnp.arange(PIECES, dtype=jnp.int32)[None, None, :], axis=2))
    column = (owner_ids[None, :, None] * PIECES + picked[:, :, None]) * PIECE + jnp.arange(PIECE, dtype=jnp.int32)[None, None, :]
    gathered = jnp.take(projected, column.reshape(-1).astype(jnp.int32), axis=1)
    live_columns = jnp.broadcast_to(slot_live[:, :, None], column.shape).reshape(-1)
    return jnp.where(live_columns[None, :], gathered, jnp.zeros((), jnp.bfloat16))
```

```python
import functools
import math

import jax
import jax.numpy as jnp
from jax import lax
from jax.experimental import pallas as pl
from jax.experimental.pallas import tpu as pltpu
from jax.sharding import PartitionSpec as P

HEAD_SIZE = 128
PIECES = 8
PIECE = 32
NDOC = 16
N_CTX = 16
N_X = 4
ROWS = 256
HEADS = 8
BACK = 4
KEYS = (BACK + 1) * ROWS
CHUNKS = 4
CHUNK = 256
HALF = 128
MASKED = -1e30
VMEM_LIMIT = 60 * 1024 * 1024


def signal(sem, **where):
    pl.semaphore_signal(
        sem, inc=1, device_id=where, device_id_type=pl.DeviceIdType.MESH
    )


def remote(src, dst, send_sem, recv_sem, **where):
    return pltpu.make_async_remote_copy(
        src_ref=src,
        dst_ref=dst,
        send_sem=send_sem,
        recv_sem=recv_sem,
        device_id=where,
        device_id_type=pl.DeviceIdType.MESH,
    )


def attention_kernel(
    lengths, q_ref, k_ref, v_ref, o_ref, kbuf, vbuf, vt, bias, send_sem, recv_sem
):
    c = lax.axis_index("ctx")
    core = lax.rem(c, 2)
    mate = c + 1 - 2 * core

    barrier = pltpu.get_barrier_semaphore()
    signal(barrier, ctx=mate)
    for far in (2, 4):

        @pl.when(c + far < N_CTX)
        def _():
            signal(barrier, ctx=c + far)

        @pl.when(c >= far)
        def _():
            signal(barrier, ctx=c - far)

    def slot(buf, back):
        return buf.at[pl.ds((BACK - back) * ROWS, ROWS)]

    kbuf[BACK * ROWS :, :] = k_ref[...]
    vbuf[BACK * ROWS :, :] = v_ref[...]
    for back in range(1, BACK + 1):

        @pl.when(c < back)
        def _():
            at = (BACK - back) * ROWS
            kbuf[at : at + ROWS, :] = jnp.zeros((ROWS, HEAD_SIZE), jnp.bfloat16)
            vbuf[at : at + ROWS, :] = jnp.zeros((ROWS, HEAD_SIZE), jnp.bfloat16)

    pos = c * ROWS + lax.broadcasted_iota(jnp.int32, (1, ROWS), 1)
    begin = jnp.int32(0)
    low = jnp.zeros((1, ROWS), jnp.int32)
    for doc in range(NDOC):
        low = jnp.where(pos >= begin, begin, low)
        begin = begin + lengths[doc]
    for at in range(0, KEYS, ROWS):
        key_pos = (
            (c - BACK) * ROWS
            + at
            + lax.broadcasted_iota(jnp.int32, (ROWS, ROWS), 0)
        )
        allowed = (key_pos >= low) & (key_pos <= pos)
        bias[at : at + ROWS, :] = jnp.where(allowed, 0.0, MASKED)

    count = 1
    for far in (2, 4):
        count = count + (c + far < N_CTX).astype(jnp.int32)
        count = count + (c >= far).astype(jnp.int32)
    pl.semaphore_wait(barrier, count)

    def far_copies(far):
        return [
            remote(
                own,
                slot(buf, far),
                send_sem.at[far // 2 - 1, i],
                recv_sem.at[far - 1, i],
                ctx=c + far,
            )
            for i, (own, buf) in enumerate(((k_ref, kbuf), (v_ref, vbuf)))
        ]

    def mate_copies(source, back):
        return [
            remote(
                source[i],
                slot(buf, back),
                send_sem.at[2 + back // 2, i],
                recv_sem.at[back - 1, i],
                ctx=mate,
            )
            for i, buf in enumerate((kbuf, vbuf))
        ]

    first_even = mate_copies((k_ref, v_ref), 1)
    first_odd = mate_copies((slot(kbuf, 2), slot(vbuf, 2)), 1)
    second_even = mate_copies((slot(kbuf, 2), slot(vbuf, 2)), 3)
    second_odd = mate_copies((slot(kbuf, 4), slot(vbuf, 4)), 3)

    @pl.when(core == 0)
    def _():
        for copy in first_even:
            copy.start()

    for far in (2, 4):

        @pl.when(c + far < N_CTX)
        def _():
            for copy in far_copies(far):
                copy.start()

    @pl.when(c >= 2)
    def _():
        for copy in far_copies(2):
            copy.wait_recv()

        @pl.when(core == 1)
        def _():
            for copy in first_odd:
                copy.start()

        @pl.when(core == 0)
        def _():
            for copy in second_even:
                copy.start()

    @pl.when(c >= 4)
    def _():
        for copy in far_copies(4):
            copy.wait_recv()

        @pl.when(core == 1)
        def _():
            for copy in second_odd:
                copy.start()

    @pl.when(c >= 1)
    def _():
        for copy in first_odd:
            copy.wait_recv()

    @pl.when(c >= 3)
    def _():
        for copy in second_odd:
            copy.wait_recv()

    vt[...] = vbuf[...].T
    factor = math.log2(math.e) / math.sqrt(HEAD_SIZE)

    @pl.loop(0, HEADS)
    def _(head):
        at = pl.multiple_of(head * HEAD_SIZE, HEAD_SIZE)
        scores = lax.dot_general(
            kbuf[...],
            q_ref[:, pl.ds(at, HEAD_SIZE)],
            (((1,), (1,)), ((), ())),
            preferred_element_type=jnp.float32,
        )
        scores = scores + bias[...]
        top = jnp.max(scores, axis=0, keepdims=True)
        weights = jnp.exp2((scores - top) * factor)
        total = jnp.sum(weights, axis=0, keepdims=True)
        mixed = jnp.dot(
            vt[...], weights.astype(jnp.bfloat16), preferred_element_type=jnp.float32
        )
        o_ref[pl.ds(at, HEAD_SIZE), :] = (mixed / total).astype(jnp.bfloat16)

    for far in (2, 4):

        @pl.when(c + far < N_CTX)
        def _():
            for copy in far_copies(far):
                copy.wait_send()

    @pl.when(core == 0)
    def _():
        for copy in first_even:
            copy.wait_send()

        @pl.when(c >= 2)
        def _():
            for copy in second_even:
                copy.wait_send()

    @pl.when(core == 1)
    def _():
        @pl.when(c >= 2)
        def _():
            for copy in first_odd:
                copy.wait_send()

        @pl.when(c >= 4)
        def _():
            for copy in second_odd:
                copy.wait_send()


def attention(lengths, queries, keys, values):
    vmem = pl.BlockSpec(memory_space=pltpu.VMEM)
    return pl.pallas_call(
        attention_kernel,
        out_shape=jax.ShapeDtypeStruct((HEADS * HEAD_SIZE, ROWS), jnp.bfloat16),
        in_specs=[pl.BlockSpec(memory_space=pltpu.SMEM), vmem, vmem, vmem],
        out_specs=vmem,
        scratch_shapes=[
            pltpu.VMEM((KEYS, HEAD_SIZE), jnp.bfloat16),
            pltpu.VMEM((KEYS, HEAD_SIZE), jnp.bfloat16),
            pltpu.VMEM((HEAD_SIZE, KEYS), jnp.bfloat16),
            pltpu.VMEM((KEYS, ROWS), jnp.float32),
            pltpu.SemaphoreType.DMA((4, 2)),
            pltpu.SemaphoreType.DMA((4, 2)),
        ],
        compiler_params=pltpu.CompilerParams(
            collective_id=0, has_side_effects=True, vmem_limit_bytes=VMEM_LIMIT
        ),
        name="attention",
    )(lengths, queries, keys, values)


def project_kernel(
    owners,
    w_ref,
    ctx_ref,
    out_ref,
    weights,
    partial,
    far_buf,
    near_buf,
    side_buf,
    near_out,
    cross_out,
    cross_buf,
    keep,
    pick,
    slab,
    w_sem,
    far_sem,
    near_sem,
    side_sem,
    cross_sem,
    spread_sem,
):
    c = lax.axis_index("ctx")
    h = lax.axis_index("head")
    x = h // 2
    y = lax.rem(h, 2)

    def column(step):
        return lax.rem(x + step + N_X, N_X)

    def at_x(step):
        return column(step) * 2 + y

    other = x * 2 + 1 - y

    barrier = pltpu.get_barrier_semaphore()
    for step in (1, -1):
        signal(barrier, head=at_x(step))
    signal(barrier, head=other)
    for step in range(1, N_CTX):
        signal(barrier, ctx=lax.rem(c + step, N_CTX))

    def load(place, i):
        return pltpu.make_async_copy(
            w_ref.at[place, :, i], weights.at[place, i], w_sem.at[place, i]
        )

    for step in (2, 1, -1, 0):
        for i in range(CHUNKS):
            load(column(step), i).start()

    row = lax.broadcasted_iota(jnp.int32, (N_CTX * PIECE, ROWS), 0)
    col = lax.broadcasted_iota(jnp.int32, (N_CTX * PIECE, ROWS), 1)
    lane = lax.broadcasted_iota(jnp.int32, (1, ROWS), 1)
    wanted = jnp.zeros((1, ROWS), jnp.int32)
    for piece in range(PIECES):
        wanted = jnp.where(
            (lane >= piece * PIECE) & (lane < (piece + 1) * PIECE),
            owners[c * PIECES + piece] * PIECE + lane - piece * PIECE,
            wanted,
        )
    pick[...] = (row == wanted).astype(jnp.float32).astype(jnp.bfloat16)

    def multiply(step, i):
        place = column(step)
        load(place, i).wait()

        @pl.loop(0, 2)
        def _(side):
            block = jnp.dot(
                weights[place, i, side],
                ctx_ref[...],
                preferred_element_type=jnp.float32,
            ).astype(jnp.bfloat16)
            partial[place, i, 0, side] = block[:HALF]
            partial[place, i, 1, side] = block[HALF:]

    def toward(u):
        return 2 * u - 1

    def far_copy(i, u):
        return remote(
            partial.at[column(2), i, u],
            far_buf.at[i, u],
            far_sem.at[0, i, u],
            far_sem.at[1, i, u],
            head=at_x(toward(u)),
        )

    def side_copy(i, u):
        return remote(
            partial.at[column(-toward(u)), i, u],
            side_buf.at[i, u],
            side_sem.at[0, i, u],
            side_sem.at[1, i, u],
            head=at_x(-toward(u)),
        )

    def near_copy(i, u):
        return remote(
            near_out.at[i, u],
            near_buf.at[i, u],
            near_sem.at[0, i, u],
            near_sem.at[1, i, u],
            head=at_x(toward(u)),
        )

    def cross_copy(i):
        return remote(
            cross_out.at[i],
            cross_buf.at[i],
            cross_sem.at[0, i],
            cross_sem.at[1, i],
            head=other,
        )

    def spread_copy(i, step):
        place = lax.rem(c + step, N_CTX)
        return remote(
            slab.at[i, pl.ds(place * PIECE, PIECE)],
            out_ref.at[i, pl.ds(c * PIECE, PIECE)],
            spread_sem.at[0, i],
            spread_sem.at[1, i],
            ctx=place,
        )

    def own_copy(i):
        return pltpu.make_async_copy(
            slab.at[i, pl.ds(c * PIECE, PIECE)],
            out_ref.at[i, pl.ds(c * PIECE, PIECE)],
            spread_sem.at[1, i],
        )

    def far_stage(i):
        multiply(2, i)

        @pl.when(i == 0)
        def _():
            pl.semaphore_wait(barrier, 2 + 1 + N_CTX - 1)

        for u in range(2):
            far_copy(i, u).start()

    def side_stage(i):
        multiply(1, i)
        side_copy(i, 0).start()
        multiply(-1, i)
        side_copy(i, 1).start()

    def near_stage(i):
        for u in range(2):
            far_copy(i, u).wait_recv()
            near_out[i, u] = (
                partial[column(toward(u)), i, u].astype(jnp.float32)
                + far_buf[i, u].astype(jnp.float32)
            ).astype(jnp.bfloat16)
            near_copy(i, u).start()

    def own_stage(i):
        multiply(0, i)
        for u in range(2):
            side_copy(i, u).wait_recv()
            near_copy(i, u).wait_recv()

            def total(side):
                return (
                    partial[x, i, u, side].astype(jnp.float32)
                    + near_buf[i, u, side].astype(jnp.float32)
                    + side_buf[i, u, side].astype(jnp.float32)
                )

            cross_out[i, u] = total(1 - y).astype(jnp.bfloat16)
            keep[i, u] = total(y)
        cross_copy(i).start()

    def last_stage(i):
        cross_copy(i).wait_recv()
        for u in range(2):
            done = (keep[i, u] + cross_buf[i, u].astype(jnp.float32)).astype(
                jnp.bfloat16
            )
            slab[i, :, u * HALF : (u + 1) * HALF] = lax.dot_general(
                pick[...],
                done,
                (((1,), (1,)), ((), ())),
                preferred_element_type=jnp.float32,
            ).astype(jnp.bfloat16)
        own_copy(i).start()
        for step in range(1, N_CTX):
            spread_copy(i, step).start()

    stages = ((far_stage, 0), (side_stage, 1), (near_stage, 2), (own_stage, 4), (last_stage, 5))

    @pl.loop(0, CHUNKS + 5)
    def _(t):
        for stage, delay in stages:

            @pl.when((t >= delay) & (t < delay + CHUNKS))
            def _():
                stage(t - delay)

    @pl.loop(0, CHUNKS)
    def _(i):
        for u in range(2):
            far_copy(i, u).wait_send()
            side_copy(i, u).wait_send()
            near_copy(i, u).wait_send()
        cross_copy(i).wait_send()
        sent = slab.at[i, pl.ds(0, (N_CTX - 1) * PIECE)]
        pltpu.make_async_copy(sent, sent, spread_sem.at[0, i]).wait()
        pltpu.make_async_copy(out_ref.at[i], out_ref.at[i], spread_sem.at[1, i]).wait()


def project(owners, out_weight, context):
    vmem = pl.BlockSpec(memory_space=pltpu.VMEM)
    hbm = pl.BlockSpec(memory_space=pl.ANY)
    slots = N_CTX * PIECE
    unit = (CHUNKS, 2, 2, HALF, ROWS)
    half_unit = (CHUNKS, 2, HALF, ROWS)
    dma = pltpu.SemaphoreType.DMA
    return pl.pallas_call(
        project_kernel,
        out_shape=jax.ShapeDtypeStruct((CHUNKS, slots, CHUNK), jnp.bfloat16),
        in_specs=[pl.BlockSpec(memory_space=pltpu.SMEM), hbm, vmem],
        out_specs=hbm,
        scratch_shapes=[
            pltpu.VMEM((N_X, CHUNKS, 2, CHUNK, HEADS * HEAD_SIZE), jnp.bfloat16),
            pltpu.VMEM((N_X,) + unit, jnp.bfloat16),
            pltpu.VMEM(unit, jnp.bfloat16),
            pltpu.VMEM(unit, jnp.bfloat16),
            pltpu.VMEM(unit, jnp.bfloat16),
            pltpu.VMEM(unit, jnp.bfloat16),
            pltpu.VMEM(half_unit, jnp.bfloat16),
            pltpu.VMEM(half_unit, jnp.bfloat16),
            pltpu.VMEM(half_unit, jnp.float32),
            pltpu.VMEM((slots, ROWS), jnp.bfloat16),
            pltpu.VMEM((CHUNKS, slots, CHUNK), jnp.bfloat16),
            dma((N_X, CHUNKS)),
            dma((2, CHUNKS, 2)),
            dma((2, CHUNKS, 2)),
            dma((2, CHUNKS, 2)),
            dma((2, CHUNKS)),
            dma((2, CHUNKS)),
        ],
        compiler_params=pltpu.CompilerParams(
            collective_id=1, has_side_effects=True, vmem_limit_bytes=VMEM_LIMIT
        ),
        name="project",
    )(owners, out_weight, context)


def per_device(queries, keys, values, out_weight, doc_lengths, owners):
    context = attention(doc_lengths, queries, keys, values)
    blocks = out_weight.reshape(N_X, 2, CHUNKS, CHUNK, out_weight.shape[1])
    arrived = project(owners[:, 0], blocks, context)
    return jnp.swapaxes(arrived, 1, 2).reshape(CHUNKS * CHUNK, N_CTX * PIECE)


def solution(mesh):
    in_specs = (P("ctx", "head"), P("ctx", "head"), P("ctx", "head"), P(None, "head"), P(), P())
    out_specs = P("head", "ctx")
    return jax.shard_map(
        per_device, mesh=mesh, in_specs=in_specs, out_specs=out_specs, check_vma=False
    )
```

```python
import functools
import math

import jax
import jax.numpy as jnp
from jax import lax
from jax.experimental import pallas as pl
from jax.experimental.pallas import tpu as pltpu
from jax.sharding import PartitionSpec as P

HEAD_SIZE = 128
PIECES = 8
PIECE = 32
NDOC = 16
N_CTX = 16
N_X = 4
ROWS = 256
HEADS = 8
BACK = 4
EARLY = 5
KEYS = (BACK + 1) * ROWS
CHUNKS = 8
CHUNK = 128
HALF = 64
MASKED = -1e30
VMEM_LIMIT = 60 * 1024 * 1024


def signal(sem, **where):
    pl.semaphore_signal(
        sem, inc=1, device_id=where, device_id_type=pl.DeviceIdType.MESH
    )


def remote(src, dst, send_sem, recv_sem, **where):
    return pltpu.make_async_remote_copy(
        src_ref=src,
        dst_ref=dst,
        send_sem=send_sem,
        recv_sem=recv_sem,
        device_id=where,
        device_id_type=pl.DeviceIdType.MESH,
    )


def attention_kernel(
    lengths,
    q_ref,
    k_ref,
    v_ref,
    o_ref,
    kbuf,
    vbuf,
    vt,
    bias,
    tops,
    totals,
    mixes,
    send_sem,
    recv_sem,
):
    c = lax.axis_index("ctx")
    core = lax.rem(c, 2)
    mate = c + 1 - 2 * core

    barrier = pltpu.get_barrier_semaphore()
    signal(barrier, ctx=mate)

    @pl.when(c + 2 < N_CTX)
    def _():
        signal(barrier, ctx=c + 2)

    @pl.when(c >= 2)
    def _():
        signal(barrier, ctx=c - 2)

    def slot(buf, back):
        return buf.at[pl.ds((BACK - back) * ROWS, ROWS)]

    kbuf[BACK * ROWS :, :] = k_ref[...]
    vbuf[BACK * ROWS :, :] = v_ref[...]
    for back in range(1, BACK + 1):

        @pl.when(c < back)
        def _():
            at = (BACK - back) * ROWS
            kbuf[at : at + ROWS, :] = jnp.zeros((ROWS, HEAD_SIZE), jnp.bfloat16)
            vbuf[at : at + ROWS, :] = jnp.zeros((ROWS, HEAD_SIZE), jnp.bfloat16)

    pos = c * ROWS + lax.broadcasted_iota(jnp.int32, (1, ROWS), 1)
    begin = jnp.int32(0)
    low = jnp.zeros((1, ROWS), jnp.int32)
    for doc in range(NDOC):
        low = jnp.where(pos >= begin, begin, low)
        begin = begin + lengths[doc]
    for at in range(0, KEYS, ROWS):
        key_pos = (
            (c - BACK) * ROWS
            + at
            + lax.broadcasted_iota(jnp.int32, (ROWS, ROWS), 0)
        )
        allowed = (key_pos >= low) & (key_pos <= pos)
        bias[at : at + ROWS, :] = jnp.where(allowed, 0.0, MASKED)

    forward = c + 2 < N_CTX
    relayed = (c >= 2) & forward
    count = 1 + forward.astype(jnp.int32) + (c >= 2).astype(jnp.int32)
    pl.semaphore_wait(barrier, count)

    def next_copies(source, back):
        return [
            remote(
                source[i],
                slot(buf, back),
                send_sem.at[back // 2 - 1, i],
                recv_sem.at[back - 1, i],
                ctx=c + 2,
            )
            for i, buf in enumerate((kbuf, vbuf))
        ]

    def mate_copies(source, back):
        return [
            remote(
                source[i],
                slot(buf, back),
                send_sem.at[2 + back // 2, i],
                recv_sem.at[back - 1, i],
                ctx=mate,
            )
            for i, buf in enumerate((kbuf, vbuf))
        ]

    near_blocks = (slot(kbuf, 2), slot(vbuf, 2))
    own_next = next_copies((k_ref, v_ref), 2)
    relay_next = next_copies(near_blocks, 4)
    first_even = mate_copies((k_ref, v_ref), 1)
    first_odd = mate_copies(near_blocks, 1)
    second_even = mate_copies(near_blocks, 3)
    second_odd = mate_copies((slot(kbuf, 4), slot(vbuf, 4)), 3)

    @pl.when(forward)
    def _():
        for copy in own_next:
            copy.start()

    @pl.when(core == 0)
    def _():
        for copy in first_even:
            copy.start()

    factor = math.log2(math.e) / math.sqrt(HEAD_SIZE)

    def turn(low_key, high_key):
        vt[:, low_key:high_key] = vbuf[low_key:high_key, :].T

    def attend(low_key, high_key, heads, first=False, last=False):
        @pl.loop(*heads)
        def _(head):
            at = pl.multiple_of(head * HEAD_SIZE, HEAD_SIZE)
            scores = lax.dot_general(
                kbuf[low_key:high_key, :],
                q_ref[:, pl.ds(at, HEAD_SIZE)],
                (((1,), (1,)), ((), ())),
                preferred_element_type=jnp.float32,
            )
            scores = scores + bias[low_key:high_key, :]
            top = jnp.max(scores, axis=0, keepdims=True)
            if not first:
                top = jnp.maximum(top, tops[head])
            weights = jnp.exp2((scores - top) * factor)
            total = jnp.sum(weights, axis=0, keepdims=True)
            mixed = jnp.dot(
                vt[:, low_key:high_key],
                weights.astype(jnp.bfloat16),
                preferred_element_type=jnp.float32,
            )
            if not first:
                shrink = jnp.exp2((tops[head] - top) * factor)
                total = total + totals[head] * shrink
                mixed = mixed + mixes[head] * shrink
            if last:
                o_ref[pl.ds(at, HEAD_SIZE), :] = (mixed / total).astype(jnp.bfloat16)
            else:
                tops[head] = top
                totals[head] = total
                mixes[head] = mixed

    turn(BACK * ROWS, KEYS)
    attend(BACK * ROWS, KEYS, (0, HEADS), first=True)

    @pl.when(c >= 2)
    def _():
        for i in range(2):
            own_next[i].wait_recv()

            @pl.when(forward)
            def _():
                relay_next[i].start()

            @pl.when(core == 1)
            def _():
                first_odd[i].start()

            @pl.when(core == 0)
            def _():
                second_even[i].start()

    @pl.when(c >= 1)
    def _():
        for copy in first_odd:
            copy.wait_recv()

    turn(2 * ROWS, BACK * ROWS)
    attend(2 * ROWS, BACK * ROWS, (0, EARLY))

    @pl.when(c >= 4)
    def _():
        for i in range(2):
            relay_next[i].wait_recv()

            @pl.when(core == 1)
            def _():
                second_odd[i].start()

    attend(2 * ROWS, BACK * ROWS, (EARLY, HEADS))

    @pl.when(c >= 3)
    def _():
        for copy in second_odd:
            copy.wait_recv()

    turn(0, 2 * ROWS)
    attend(0, 2 * ROWS, (0, HEADS), last=True)

    @pl.when(forward)
    def _():
        for copy in own_next:
            copy.wait_send()

    @pl.when(relayed)
    def _():
        for copy in relay_next:
            copy.wait_send()

    @pl.when(core == 0)
    def _():
        for copy in first_even:
            copy.wait_send()

        @pl.when(c >= 2)
        def _():
            for copy in second_even:
                copy.wait_send()

    @pl.when(core == 1)
    def _():
        @pl.when(c >= 2)
        def _():
            for copy in first_odd:
                copy.wait_send()

        @pl.when(c >= 4)
        def _():
            for copy in second_odd:
                copy.wait_send()


def attention(lengths, queries, keys, values):
    vmem = pl.BlockSpec(memory_space=pltpu.VMEM)
    return pl.pallas_call(
        attention_kernel,
        out_shape=jax.ShapeDtypeStruct((HEADS * HEAD_SIZE, ROWS), jnp.bfloat16),
        in_specs=[pl.BlockSpec(memory_space=pltpu.SMEM), vmem, vmem, vmem],
        out_specs=vmem,
        scratch_shapes=[
            pltpu.VMEM((KEYS, HEAD_SIZE), jnp.bfloat16),
            pltpu.VMEM((KEYS, HEAD_SIZE), jnp.bfloat16),
            pltpu.VMEM((HEAD_SIZE, KEYS), jnp.bfloat16),
            pltpu.VMEM((KEYS, ROWS), jnp.float32),
            pltpu.VMEM((HEADS, 1, ROWS), jnp.float32),
            pltpu.VMEM((HEADS, 1, ROWS), jnp.float32),
            pltpu.VMEM((HEADS, HEAD_SIZE, ROWS), jnp.float32),
            pltpu.SemaphoreType.DMA((4, 2)),
            pltpu.SemaphoreType.DMA((4, 2)),
        ],
        compiler_params=pltpu.CompilerParams(
            collective_id=0, has_side_effects=True, vmem_limit_bytes=VMEM_LIMIT
        ),
        name="attention",
    )(lengths, queries, keys, values)


def project_kernel(
    owners,
    w_ref,
    ctx_ref,
    out_ref,
    weights,
    partial,
    far_buf,
    near_buf,
    side_buf,
    near_out,
    cross_out,
    cross_buf,
    keep,
    pick,
    slab,
    w_sem,
    far_sem,
    near_sem,
    side_sem,
    cross_sem,
    spread_sem,
):
    c = lax.axis_index("ctx")
    h = lax.axis_index("head")
    x = h // 2
    y = lax.rem(h, 2)

    def column(step):
        return lax.rem(x + step + N_X, N_X)

    def at_x(step):
        return column(step) * 2 + y

    other = x * 2 + 1 - y

    barrier = pltpu.get_barrier_semaphore()
    for step in (1, -1):
        signal(barrier, head=at_x(step))
    signal(barrier, head=other)
    for step in range(1, N_CTX):
        signal(barrier, ctx=lax.rem(c + step, N_CTX))

    def load(place, i):
        return pltpu.make_async_copy(
            w_ref.at[place, :, i], weights.at[place, i], w_sem.at[place, i]
        )

    for step in (2, 1, -1, 0):
        for i in range(CHUNKS):
            load(column(step), i).start()

    row = lax.broadcasted_iota(jnp.int32, (N_CTX * PIECE, ROWS), 0)
    col = lax.broadcasted_iota(jnp.int32, (N_CTX * PIECE, ROWS), 1)
    lane = lax.broadcasted_iota(jnp.int32, (1, ROWS), 1)
    wanted = jnp.zeros((1, ROWS), jnp.int32)
    for piece in range(PIECES):
        wanted = jnp.where(
            (lane >= piece * PIECE) & (lane < (piece + 1) * PIECE),
            owners[c * PIECES + piece] * PIECE + lane - piece * PIECE,
            wanted,
        )
    pick[...] = (row == wanted).astype(jnp.float32).astype(jnp.bfloat16)

    def multiply(step, i):
        place = column(step)
        load(place, i).wait()

        block = jnp.dot(
            weights[place, i].reshape(2 * CHUNK, HEADS * HEAD_SIZE),
            ctx_ref[...],
            preferred_element_type=jnp.float32,
        ).astype(jnp.bfloat16)
        for side in range(2):
            for u in range(2):
                at = side * CHUNK + u * HALF
                partial[place, i, u, side] = block[at : at + HALF]

    def toward(u):
        return 2 * u - 1

    def far_copy(i, u):
        return remote(
            partial.at[column(2), i, u],
            far_buf.at[i, u],
            far_sem.at[0, i, u],
            far_sem.at[1, i, u],
            head=at_x(toward(u)),
        )

    def side_copy(i, u):
        return remote(
            partial.at[column(-toward(u)), i, u],
            side_buf.at[i, u],
            side_sem.at[0, i, u],
            side_sem.at[1, i, u],
            head=at_x(-toward(u)),
        )

    def near_copy(i, u):
        return remote(
            near_out.at[i, u],
            near_buf.at[i, u],
            near_sem.at[0, i, u],
            near_sem.at[1, i, u],
            head=at_x(toward(u)),
        )

    def cross_copy(i):
        return remote(
            cross_out.at[i],
            cross_buf.at[i],
            cross_sem.at[0, i],
            cross_sem.at[1, i],
            head=other,
        )

    def spread_copy(i, step):
        place = lax.rem(c + step, N_CTX)
        return remote(
            slab.at[i, pl.ds(place * PIECE, PIECE)],
            out_ref.at[i, pl.ds(c * PIECE, PIECE)],
            spread_sem.at[0, i],
            spread_sem.at[1, i],
            ctx=place,
        )

    def own_copy(i):
        return pltpu.make_async_copy(
            slab.at[i, pl.ds(c * PIECE, PIECE)],
            out_ref.at[i, pl.ds(c * PIECE, PIECE)],
            spread_sem.at[1, i],
        )

    def far_stage(i):
        multiply(2, i)

        @pl.when(i == 0)
        def _():
            pl.semaphore_wait(barrier, 2 + 1 + N_CTX - 1)

        for u in range(2):
            far_copy(i, u).start()

    def side_stage(i):
        multiply(1, i)
        side_copy(i, 0).start()
        multiply(-1, i)
        side_copy(i, 1).start()

    def near_stage(i):
        for u in range(2):
            far_copy(i, u).wait_recv()
            near_out[i, u] = (
                partial[column(toward(u)), i, u].astype(jnp.float32)
                + far_buf[i, u].astype(jnp.float32)
            ).astype(jnp.bfloat16)
            near_copy(i, u).start()

    def own_stage(i):
        multiply(0, i)
        for u in range(2):
            side_copy(i, u).wait_recv()
            near_copy(i, u).wait_recv()

            def total(side):
                return (
                    partial[x, i, u, side].astype(jnp.float32)
                    + near_buf[i, u, side].astype(jnp.float32)
                    + side_buf[i, u, side].astype(jnp.float32)
                )

            cross_out[i, u] = total(1 - y).astype(jnp.bfloat16)
            keep[i, u] = total(y)
        cross_copy(i).start()

    def last_stage(i):
        cross_copy(i).wait_recv()
        done = (keep[i] + cross_buf[i].astype(jnp.float32)).astype(jnp.bfloat16)
        slab[i] = lax.dot_general(
            pick[...],
            done.reshape(CHUNK, ROWS),
            (((1,), (1,)), ((), ())),
            preferred_element_type=jnp.float32,
        ).astype(jnp.bfloat16)
        own_copy(i).start()
        for step in range(1, N_CTX):
            spread_copy(i, step).start()

    stages = ((far_stage, 0), (side_stage, 1), (near_stage, 2), (own_stage, 4), (last_stage, 5))

    @pl.loop(0, CHUNKS + 5)
    def _(t):
        for stage, delay in stages:

            @pl.when((t >= delay) & (t < delay + CHUNKS))
            def _():
                stage(t - delay)

    @pl.loop(0, CHUNKS)
    def _(i):
        for u in range(2):
            far_copy(i, u).wait_send()
            side_copy(i, u).wait_send()
            near_copy(i, u).wait_send()
        cross_copy(i).wait_send()
        sent = slab.at[i, pl.ds(0, (N_CTX - 1) * PIECE)]
        pltpu.make_async_copy(sent, sent, spread_sem.at[0, i]).wait()
        pltpu.make_async_copy(out_ref.at[i], out_ref.at[i], spread_sem.at[1, i]).wait()


def project(owners, out_weight, context):
    vmem = pl.BlockSpec(memory_space=pltpu.VMEM)
    hbm = pl.BlockSpec(memory_space=pl.ANY)
    slots = N_CTX * PIECE
    unit = (CHUNKS, 2, 2, HALF, ROWS)
    half_unit = (CHUNKS, 2, HALF, ROWS)
    dma = pltpu.SemaphoreType.DMA
    return pl.pallas_call(
        project_kernel,
        out_shape=jax.ShapeDtypeStruct((CHUNKS, slots, CHUNK), jnp.bfloat16),
        in_specs=[pl.BlockSpec(memory_space=pltpu.SMEM), hbm, vmem],
        out_specs=hbm,
        scratch_shapes=[
            pltpu.VMEM((N_X, CHUNKS, 2, CHUNK, HEADS * HEAD_SIZE), jnp.bfloat16),
            pltpu.VMEM((N_X,) + unit, jnp.bfloat16),
            pltpu.VMEM(unit, jnp.bfloat16),
            pltpu.VMEM(unit, jnp.bfloat16),
            pltpu.VMEM(unit, jnp.bfloat16),
            pltpu.VMEM(unit, jnp.bfloat16),
            pltpu.VMEM(half_unit, jnp.bfloat16),
            pltpu.VMEM(half_unit, jnp.bfloat16),
            pltpu.VMEM(half_unit, jnp.float32),
            pltpu.VMEM((slots, ROWS), jnp.bfloat16),
            pltpu.VMEM((CHUNKS, slots, CHUNK), jnp.bfloat16),
            dma((N_X, CHUNKS)),
            dma((2, CHUNKS, 2)),
            dma((2, CHUNKS, 2)),
            dma((2, CHUNKS, 2)),
            dma((2, CHUNKS)),
            dma((2, CHUNKS)),
        ],
        compiler_params=pltpu.CompilerParams(
            collective_id=1, has_side_effects=True, vmem_limit_bytes=VMEM_LIMIT
        ),
        name="project",
    )(owners, out_weight, context)


def per_device(queries, keys, values, out_weight, doc_lengths, owners):
    context = attention(doc_lengths, queries, keys, values)
    blocks = out_weight.reshape(N_X, 2, CHUNKS, CHUNK, out_weight.shape[1])
    arrived = project(owners[:, 0], blocks, context)
    return jnp.swapaxes(arrived, 1, 2).reshape(CHUNKS * CHUNK, N_CTX * PIECE)


def solution(mesh):
    in_specs = (P("ctx", "head"), P("ctx", "head"), P("ctx", "head"), P(None, "head"), P(), P())
    out_specs = P("head", "ctx")
    return jax.shard_map(
        per_device, mesh=mesh, in_specs=in_specs, out_specs=out_specs, check_vma=False
    )
```

```python
import functools
import math

import jax
import jax.numpy as jnp
from jax import lax
from jax.experimental import pallas as pl
from jax.experimental.pallas import tpu as pltpu
from jax.sharding import PartitionSpec as P

HEAD_SIZE = 128
PIECES = 8
PIECE = 32
NDOC = 16
N_CTX = 16
N_X = 4
ROWS = 256
HEADS = 8
BACK = 4
EARLY = 5
KEYS = (BACK + 1) * ROWS
CHUNKS = 8
CHUNK = 128
HALF = 64
MASKED = -1e30
VMEM_LIMIT = 60 * 1024 * 1024


def signal(sem, **where):
    pl.semaphore_signal(
        sem, inc=1, device_id=where, device_id_type=pl.DeviceIdType.MESH
    )


def remote(src, dst, send_sem, recv_sem, **where):
    return pltpu.make_async_remote_copy(
        src_ref=src,
        dst_ref=dst,
        send_sem=send_sem,
        recv_sem=recv_sem,
        device_id=where,
        device_id_type=pl.DeviceIdType.MESH,
    )


def attend_rows(
    lengths,
    prepare,
    q_ref,
    k_ref,
    v_ref,
    o_ref,
    kbuf,
    vbuf,
    vt,
    bias,
    tops,
    totals,
    mixes,
    send_sem,
    recv_sem,
):
    c = lax.axis_index("ctx")
    core = lax.rem(c, 2)
    mate = c + 1 - 2 * core

    def slot(buf, back):
        return buf.at[pl.ds((BACK - back) * ROWS, ROWS)]

    kbuf[BACK * ROWS :, :] = k_ref[...]
    vbuf[BACK * ROWS :, :] = v_ref[...]
    for back in range(1, BACK + 1):

        @pl.when(c < back)
        def _():
            at = (BACK - back) * ROWS
            kbuf[at : at + ROWS, :] = jnp.zeros((ROWS, HEAD_SIZE), jnp.bfloat16)
            vbuf[at : at + ROWS, :] = jnp.zeros((ROWS, HEAD_SIZE), jnp.bfloat16)

    pos = c * ROWS + lax.broadcasted_iota(jnp.int32, (1, ROWS), 1)
    begin = jnp.int32(0)
    low = jnp.zeros((1, ROWS), jnp.int32)
    for doc in range(NDOC):
        low = jnp.where(pos >= begin, begin, low)
        begin = begin + lengths[doc]
    for at in range(0, KEYS, ROWS):
        key_pos = (
            (c - BACK) * ROWS
            + at
            + lax.broadcasted_iota(jnp.int32, (ROWS, ROWS), 0)
        )
        allowed = (key_pos >= low) & (key_pos <= pos)
        bias[at : at + ROWS, :] = jnp.where(allowed, 0.0, MASKED)

    forward = c + 2 < N_CTX
    relayed = (c >= 2) & forward
    prepare()

    def next_copies(source, back):
        return [
            remote(
                source[i],
                slot(buf, back),
                send_sem.at[back // 2 - 1, i],
                recv_sem.at[back - 1, i],
                ctx=c + 2,
            )
            for i, buf in enumerate((kbuf, vbuf))
        ]

    def mate_copies(source, back):
        return [
            remote(
                source[i],
                slot(buf, back),
                send_sem.at[2 + back // 2, i],
                recv_sem.at[back - 1, i],
                ctx=mate,
            )
            for i, buf in enumerate((kbuf, vbuf))
        ]

    near_blocks = (slot(kbuf, 2), slot(vbuf, 2))
    own_next = next_copies((k_ref, v_ref), 2)
    relay_next = next_copies(near_blocks, 4)
    first_even = mate_copies((k_ref, v_ref), 1)
    first_odd = mate_copies(near_blocks, 1)
    second_even = mate_copies(near_blocks, 3)
    second_odd = mate_copies((slot(kbuf, 4), slot(vbuf, 4)), 3)

    @pl.when(forward)
    def _():
        for copy in own_next:
            copy.start()

    @pl.when(core == 0)
    def _():
        for copy in first_even:
            copy.start()

    factor = math.log2(math.e) / math.sqrt(HEAD_SIZE)

    def turn(low_key, high_key):
        vt[:, low_key:high_key] = vbuf[low_key:high_key, :].T

    def attend(low_key, high_key, heads, first=False, last=False):
        @pl.loop(*heads)
        def _(head):
            at = pl.multiple_of(head * HEAD_SIZE, HEAD_SIZE)
            scores = lax.dot_general(
                kbuf[low_key:high_key, :],
                q_ref[:, pl.ds(at, HEAD_SIZE)],
                (((1,), (1,)), ((), ())),
                preferred_element_type=jnp.float32,
            )
            scores = scores + bias[low_key:high_key, :]
            top = jnp.max(scores, axis=0, keepdims=True)
            if not first:
                top = jnp.maximum(top, tops[head])
            weights = jnp.exp2((scores - top) * factor)
            total = jnp.sum(weights, axis=0, keepdims=True)
            mixed = jnp.dot(
                vt[:, low_key:high_key],
                weights.astype(jnp.bfloat16),
                preferred_element_type=jnp.float32,
            )
            if not first:
                shrink = jnp.exp2((tops[head] - top) * factor)
                total = total + totals[head] * shrink
                mixed = mixed + mixes[head] * shrink
            if last:
                o_ref[pl.ds(at, HEAD_SIZE), :] = (mixed / total).astype(jnp.bfloat16)
            else:
                tops[head] = top
                totals[head] = total
                mixes[head] = mixed

    turn(BACK * ROWS, KEYS)
    attend(BACK * ROWS, KEYS, (0, HEADS), first=True)

    @pl.when(c >= 2)
    def _():
        for i in range(2):
            own_next[i].wait_recv()

            @pl.when(forward)
            def _():
                relay_next[i].start()

            @pl.when(core == 1)
            def _():
                first_odd[i].start()

            @pl.when(core == 0)
            def _():
                second_even[i].start()

    @pl.when(c >= 1)
    def _():
        for copy in first_odd:
            copy.wait_recv()

    turn(2 * ROWS, BACK * ROWS)
    attend(2 * ROWS, BACK * ROWS, (0, EARLY))

    @pl.when(c >= 4)
    def _():
        for i in range(2):
            relay_next[i].wait_recv()

            @pl.when(core == 1)
            def _():
                second_odd[i].start()

    attend(2 * ROWS, BACK * ROWS, (EARLY, HEADS))

    @pl.when(c >= 3)
    def _():
        for copy in second_odd:
            copy.wait_recv()

    turn(0, 2 * ROWS)
    attend(0, 2 * ROWS, (0, HEADS), last=True)

    @pl.when(forward)
    def _():
        for copy in own_next:
            copy.wait_send()

    @pl.when(relayed)
    def _():
        for copy in relay_next:
            copy.wait_send()

    @pl.when(core == 0)
    def _():
        for copy in first_even:
            copy.wait_send()

        @pl.when(c >= 2)
        def _():
            for copy in second_even:
                copy.wait_send()

    @pl.when(core == 1)
    def _():
        @pl.when(c >= 2)
        def _():
            for copy in first_odd:
                copy.wait_send()

        @pl.when(c >= 4)
        def _():
            for copy in second_odd:
                copy.wait_send()


def layer_kernel(
    lengths,
    owners,
    q_ref,
    k_ref,
    v_ref,
    w_ref,
    out_ref,
    ctx_ref,
    kbuf,
    vbuf,
    vt,
    bias,
    tops,
    totals,
    mixes,
    send_sem,
    recv_sem,
    weights,
    partial,
    far_buf,
    near_buf,
    side_buf,
    near_out,
    cross_out,
    cross_buf,
    keep,
    pick,
    slab,
    w_sem,
    far_sem,
    near_sem,
    side_sem,
    cross_sem,
    spread_sem,
):
    c = lax.axis_index("ctx")
    h = lax.axis_index("head")
    x = h // 2
    y = lax.rem(h, 2)

    def column(step):
        return lax.rem(x + step + N_X, N_X)

    def at_x(step):
        return column(step) * 2 + y

    other = x * 2 + 1 - y

    barrier = pltpu.get_barrier_semaphore()
    for step in (1, -1):
        signal(barrier, head=at_x(step))
    signal(barrier, head=other)
    for step in range(1, N_CTX):
        signal(barrier, ctx=lax.rem(c + step, N_CTX))

    def load(place, i):
        return pltpu.make_async_copy(
            w_ref.at[place, :, i], weights.at[place, i], w_sem.at[place, i]
        )

    for step in (2, 1, -1, 0):
        for i in range(CHUNKS):
            load(column(step), i).start()

    def prepare():
        row = lax.broadcasted_iota(jnp.int32, (N_CTX * PIECE, ROWS), 0)
        col = lax.broadcasted_iota(jnp.int32, (N_CTX * PIECE, ROWS), 1)
        lane = lax.broadcasted_iota(jnp.int32, (1, ROWS), 1)
        wanted = jnp.zeros((1, ROWS), jnp.int32)
        for piece in range(PIECES):
            wanted = jnp.where(
                (lane >= piece * PIECE) & (lane < (piece + 1) * PIECE),
                owners[c * PIECES + piece] * PIECE + lane - piece * PIECE,
                wanted,
            )
        pick[...] = (row == wanted).astype(jnp.float32).astype(jnp.bfloat16)
        pl.semaphore_wait(barrier, 2 + 1 + N_CTX - 1)

    attend_rows(
        lengths,
        prepare,
        q_ref,
        k_ref,
        v_ref,
        ctx_ref,
        kbuf,
        vbuf,
        vt,
        bias,
        tops,
        totals,
        mixes,
        send_sem,
        recv_sem,
    )

    def multiply(step, i):
        place = column(step)
        load(place, i).wait()

        block = jnp.dot(
            weights[place, i].reshape(2 * CHUNK, HEADS * HEAD_SIZE),
            ctx_ref[...],
            preferred_element_type=jnp.float32,
        ).astype(jnp.bfloat16)
        for side in range(2):
            for u in range(2):
                at = side * CHUNK + u * HALF
                partial[place, i, u, side] = block[at : at + HALF]

    def toward(u):
        return 2 * u - 1

    def far_copy(i, u):
        return remote(
            partial.at[column(2), i, u],
            far_buf.at[i, u],
            far_sem.at[0, i, u],
            far_sem.at[1, i, u],
            head=at_x(toward(u)),
        )

    def side_copy(i, u):
        return remote(
            partial.at[column(-toward(u)), i, u],
            side_buf.at[i, u],
            side_sem.at[0, i, u],
            side_sem.at[1, i, u],
            head=at_x(-toward(u)),
        )

    def near_copy(i, u):
        return remote(
            near_out.at[i, u],
            near_buf.at[i, u],
            near_sem.at[0, i, u],
            near_sem.at[1, i, u],
            head=at_x(toward(u)),
        )

    def cross_copy(i):
        return remote(
            cross_out.at[i],
            cross_buf.at[i],
            cross_sem.at[0, i],
            cross_sem.at[1, i],
            head=other,
        )

    def spread_copy(i, step):
        place = lax.rem(c + step, N_CTX)
        return remote(
            slab.at[i, pl.ds(place * PIECE, PIECE)],
            out_ref.at[i, pl.ds(c * PIECE, PIECE)],
            spread_sem.at[0, i],
            spread_sem.at[1, i],
            ctx=place,
        )

    def own_copy(i):
        return pltpu.make_async_copy(
            slab.at[i, pl.ds(c * PIECE, PIECE)],
            out_ref.at[i, pl.ds(c * PIECE, PIECE)],
            spread_sem.at[1, i],
        )

    def far_stage(i):
        multiply(2, i)
        for u in range(2):
            far_copy(i, u).start()

    def side_stage(i):
        multiply(1, i)
        side_copy(i, 0).start()
        multiply(-1, i)
        side_copy(i, 1).start()

    def near_stage(i):
        for u in range(2):
            far_copy(i, u).wait_recv()
            near_out[i, u] = (
                partial[column(toward(u)), i, u].astype(jnp.float32)
                + far_buf[i, u].astype(jnp.float32)
            ).astype(jnp.bfloat16)
            near_copy(i, u).start()

    def own_stage(i):
        multiply(0, i)
        for u in range(2):
            side_copy(i, u).wait_recv()
            near_copy(i, u).wait_recv()

            def total(side):
                return (
                    partial[x, i, u, side].astype(jnp.float32)
                    + near_buf[i, u, side].astype(jnp.float32)
                    + side_buf[i, u, side].astype(jnp.float32)
                )

            cross_out[i, u] = total(1 - y).astype(jnp.bfloat16)
            keep[i, u] = total(y)
        cross_copy(i).start()

    def last_stage(i):
        cross_copy(i).wait_recv()
        done = (keep[i] + cross_buf[i].astype(jnp.float32)).astype(jnp.bfloat16)
        slab[i] = lax.dot_general(
            pick[...],
            done.reshape(CHUNK, ROWS),
            (((1,), (1,)), ((), ())),
            preferred_element_type=jnp.float32,
        ).astype(jnp.bfloat16)
        own_copy(i).start()
        for step in range(1, N_CTX):
            spread_copy(i, step).start()

    stages = ((far_stage, 0), (side_stage, 1), (near_stage, 2), (own_stage, 4), (last_stage, 5))

    @pl.loop(0, CHUNKS + 5)
    def _(t):
        for stage, delay in stages:

            @pl.when((t >= delay) & (t < delay + CHUNKS))
            def _():
                stage(t - delay)

    @pl.loop(0, CHUNKS)
    def _(i):
        for u in range(2):
            far_copy(i, u).wait_send()
            side_copy(i, u).wait_send()
            near_copy(i, u).wait_send()
        cross_copy(i).wait_send()
        sent = slab.at[i, pl.ds(0, (N_CTX - 1) * PIECE)]
        pltpu.make_async_copy(sent, sent, spread_sem.at[0, i]).wait()
        pltpu.make_async_copy(out_ref.at[i], out_ref.at[i], spread_sem.at[1, i]).wait()


def layer(lengths, owners, queries, keys, values, out_weight):
    vmem = pl.BlockSpec(memory_space=pltpu.VMEM)
    hbm = pl.BlockSpec(memory_space=pl.ANY)
    smem = pl.BlockSpec(memory_space=pltpu.SMEM)
    slots = N_CTX * PIECE
    unit = (CHUNKS, 2, 2, HALF, ROWS)
    half_unit = (CHUNKS, 2, HALF, ROWS)
    dma = pltpu.SemaphoreType.DMA
    return pl.pallas_call(
        layer_kernel,
        out_shape=jax.ShapeDtypeStruct((CHUNKS, slots, CHUNK), jnp.bfloat16),
        in_specs=[smem, smem, vmem, vmem, vmem, hbm],
        out_specs=hbm,
        scratch_shapes=[
            pltpu.VMEM((HEADS * HEAD_SIZE, ROWS), jnp.bfloat16),
            pltpu.VMEM((KEYS, HEAD_SIZE), jnp.bfloat16),
            pltpu.VMEM((KEYS, HEAD_SIZE), jnp.bfloat16),
            pltpu.VMEM((HEAD_SIZE, KEYS), jnp.bfloat16),
            pltpu.VMEM((KEYS, ROWS), jnp.float32),
            pltpu.VMEM((HEADS, 1, ROWS), jnp.float32),
            pltpu.VMEM((HEADS, 1, ROWS), jnp.float32),
            pltpu.VMEM((HEADS, HEAD_SIZE, ROWS), jnp.float32),
            dma((4, 2)),
            dma((4, 2)),
            pltpu.VMEM((N_X, CHUNKS, 2, CHUNK, HEADS * HEAD_SIZE), jnp.bfloat16),
            pltpu.VMEM((N_X,) + unit, jnp.bfloat16),
            pltpu.VMEM(unit, jnp.bfloat16),
            pltpu.VMEM(unit, jnp.bfloat16),
            pltpu.VMEM(unit, jnp.bfloat16),
            pltpu.VMEM(unit, jnp.bfloat16),
            pltpu.VMEM(half_unit, jnp.bfloat16),
            pltpu.VMEM(half_unit, jnp.bfloat16),
            pltpu.VMEM(half_unit, jnp.float32),
            pltpu.VMEM((slots, ROWS), jnp.bfloat16),
            pltpu.VMEM((CHUNKS, slots, CHUNK), jnp.bfloat16),
            dma((N_X, CHUNKS)),
            dma((2, CHUNKS, 2)),
            dma((2, CHUNKS, 2)),
            dma((2, CHUNKS, 2)),
            dma((2, CHUNKS)),
            dma((2, CHUNKS)),
        ],
        compiler_params=pltpu.CompilerParams(
            collective_id=0, has_side_effects=True, vmem_limit_bytes=VMEM_LIMIT
        ),
        name="layer",
    )(lengths, owners, queries, keys, values, out_weight)


def per_device(queries, keys, values, out_weight, doc_lengths, owners):
    blocks = out_weight.reshape(N_X, 2, CHUNKS, CHUNK, out_weight.shape[1])
    arrived = layer(doc_lengths, owners[:, 0], queries, keys, values, blocks)
    return jnp.swapaxes(arrived, 1, 2).reshape(CHUNKS * CHUNK, N_CTX * PIECE)


def solution(mesh):
    in_specs = (P("ctx", "head"), P("ctx", "head"), P("ctx", "head"), P(None, "head"), P(), P())
    out_specs = P("head", "ctx")
    return jax.shard_map(
        per_device, mesh=mesh, in_specs=in_specs, out_specs=out_specs, check_vma=False
    )
```
